32 devices in a mesh: grp: 4 (over z), dev: 8 (over y, x, core).
Axes of the slice: x: 2, y: 2, z: 4, core: 2. Of those that a mesh axis runs over, the one named last changes fastest.
Arguments:
- panel: float32 [32768, 512], P(('grp', 'dev')), may hold values from -45 to 45
- signs: int32 [32768], P(('grp', 'dev')), may hold values from 0 to 1
- source_group: int32 [4, 8, 32, 1], P(None, 'dev'), may hold values from 0 to 3; in each aligned block of 32 rows (0 to 31, 32 to 63, ..., all dimensions but the last counted through in order) at most 16 rows name the same one
- source_row: int32 [4, 8, 32], P(None, 'dev'), may hold values from 0 to 1023, as said below
Outputs:
- sketch: float32 [1024, 512], P(('grp', 'dev'))
- conditioned: float32 [32768, 512], P(('grp', 'dev'))
The draws below stay inside these ranges and needn't reach their ends.
Inputs may be any that keep to these rules, and one draw needn't show every extreme that they name: Among the 32 entries source_group[g, d, :, 0] for one g and d, no group is named more than 16 times, and in some such block one group is named exactly 16 times. source_row[g, d, j] lies in the row band of owner j // 4: source_row[g, d, j] // 128 equals j // 4; the row within the band is free.
All inputs are finite; a program needn't handle non-finite values.
Results may differ from the reference program's by a relative error of at most 0.00013.
Values sent between devices are 32-bit elements; how exact they have to be, the bound alone decides.
A program may use at most 64 MiB of HBM per device.

```python
import math
import jax
import jax.numpy as jnp
import numpy as np
from jax import lax

COLUMNS = 512
ROWS_DEV = 1024
PICKS_PER = 4
CAPACITY = 16
SKETCH_ROWS = 1024
PANEL_ROWS = 32768
N_GRP = 4
N_DEV = 8


def draw_panel(key, part):
    row_key = jax.random.fold_in(key, 11)
    col_key = jax.random.fold_in(key, 12)
    base_key = jax.random.fold_in(key, 13)
    row_scale = 0.3 * jnp.exp(jax.random.uniform(row_key, (PANEL_ROWS, 1), minval=0.0, maxval=math.log(10.0)))
    col_scale = 0.3 * jnp.exp(jax.random.uniform(col_key, (1, COLUMNS), minval=0.0, maxval=math.log(10.0)))
    base = jnp.clip(jax.random.normal(base_key, (PANEL_ROWS, COLUMNS)), -5.0, 5.0)
    values = base * row_scale * col_scale
    return values.astype(jnp.float32)


def draw_source_row(key, part):
    band_size = ROWS_DEV // N_DEV
    width = N_DEV * PICKS_PER
    offset_key = jax.random.fold_in(key, 21)
    offset = jax.random.randint(offset_key, (N_GRP, N_DEV, width), 0, band_size)
    flat_place = jnp.arange(N_GRP * N_DEV * width, dtype=jnp.int32).reshape(N_GRP, N_DEV, width)
    offset = jnp.where(flat_place == 0, 0, offset)
    offset = jnp.where(flat_place == N_GRP * N_DEV * width - 1, band_size - 1, offset)
    band = jnp.arange(width, dtype=jnp.int32) // PICKS_PER * band_size
    return (band[None, None, :] + offset).astype(jnp.int32)


def set_ends(values, key, least, largest):
    spot = [jax.random.randint(jax.random.fold_in(key, axis), (), 0, length) for axis, length in enumerate(values.shape)]
    main_axis = values.shape.index(max(values.shape))
    beside = spot[:main_axis] + [(spot[main_axis] + 1) % values.shape[main_axis]] + spot[main_axis + 1:]
    return values.at[tuple(spot)].set(least).at[tuple(beside)].set(largest)


def deal_out(rng, own, number, rows, number_of, top, reach, skew):
    sequence = jax.random.permutation(rng, number_of)
    packed, usual = shares(number_of, rows * top, reach, skew, True), shares(number_of, rows * top, reach, skew, False)
    places = jnp.arange(number_of)

    def named(sizes, rotation):
        used = int((sizes > 0).sum())
        fixed = max(1, used // 4)
        shifted = fixed + (places - fixed + rotation * (used - fixed)) % max(1, number_of - fixed)
        return jnp.zeros((number_of,), jnp.int32).at[sequence[jnp.where(places < fixed, places, shifted)]].set(jnp.asarray(sizes, jnp.int32))

    sizes = jnp.where(number % 4 == 0, named(packed, number // 4), named(usual, number - number // 4 - 1))
    mixed = jax.random.permutation(jax.random.fold_in(own, 3), number_of)
    donor, receiver = mixed[0:number_of // 2 * 2:2], mixed[1:number_of // 2 * 2:2]
    slack = jnp.minimum(sizes[donor] - 1, reach - sizes[receiver]) // 2
    slack = jnp.where((donor == sequence[0]) | (receiver == sequence[0]) | (sizes[receiver] == 0), 0, jnp.maximum(slack, 0))
    shifted = jax.random.randint(jax.random.fold_in(own, 4), (number_of // 2,), 0, 1 << 20) % (slack + 1)
    sizes = sizes.at[donor].add(-shifted).at[receiver].add(shifted)
    items = jnp.searchsorted(jnp.cumsum(sizes), jnp.arange(rows * top), side="right").astype(jnp.int32)
    table = items.reshape(top, rows).T
    table = table[jax.random.permutation(jax.random.fold_in(own, 1), rows)]
    rotation = jax.random.randint(jax.random.fold_in(own, 2), (rows, 1), 0, top)
    return jnp.take_along_axis(table, (jnp.arange(top)[None, :] + rotation) % top, axis=1)


def shares(amount, total, most, lean, full):
    portions = [(1 << 20) // math.isqrt(grade ** lean) + 1 for grade in range(1, amount + 1)]
    largest = most if full else min(most, max(-(-total // amount), total * portions[0] // sum(portions)))
    least = 1 if total - largest >= amount - 1 else 0
    counts, rest = [largest] + [least] * (amount - 1), total - largest - least * (amount - 1)
    while rest > 0:
        candidates = [i for i in range(1, amount) if counts[i] < largest] or [i for i in range(1, amount) if counts[i] < most]
        pool, remaining = sum([portions[i] for i in candidates]), rest
        for i in candidates:
            extra = min(most - counts[i], max(1, remaining * portions[i] // pool), rest)
            counts[i] = counts[i] + extra
            rest = rest - extra
    return np.array(counts)


def setup_inputs(seed: int = 0) -> dict:
    splits = jax.random.split(jax.random.key(seed), 5)
    panel = draw_panel(jax.random.fold_in(splits[4], 71), 0)
    signs = set_ends(jax.random.randint(splits[1], (PANEL_ROWS,), 0, 2), jax.random.fold_in(splits[1], 1), 0, 1).astype(jnp.int32)
    source_group_keys = jax.random.split(jax.random.fold_in(splits[2], 1), N_GRP * N_DEV * (N_DEV * PICKS_PER) // (N_DEV * PICKS_PER))
    source_group_turns = jax.random.permutation(jax.random.fold_in(splits[2], 3), N_GRP * N_DEV * (N_DEV * PICKS_PER) // (N_DEV * PICKS_PER))
    source_group = jax.vmap(lambda own, number: deal_out(jax.random.fold_in(splits[2], 2), own, number, N_DEV * PICKS_PER, N_GRP, 1, CAPACITY, 2))(source_group_keys, source_group_turns).reshape((N_GRP, N_DEV, N_DEV * PICKS_PER, 1))
    source_row = draw_source_row(jax.random.fold_in(splits[4], 71), 0)
    return {"panel": panel, "signs": signs, "source_group": source_group, "source_row": source_row}


def bit_parity(value, bits):
    total = jnp.zeros_like(value)
    for bit_place in range(bits):
        total = total + (value >> bit_place & 1)
    return total & 1

def walsh(block):
    order = block.shape[0]
    result = block
    span = 1
    for level in range(int(math.log2(order))):
        shaped = result.reshape(order // (2 * span), 2, span, -1)
        upper = shaped[:, 0]
        below = shaped[:, 1]
        result = jnp.stack([upper + below, upper - below], axis=1).reshape(order, -1)
        span = span * 2
    return result

def reference(panel, signs, source_group, source_row):
    flipped = panel * (1 - 2 * signs).astype(jnp.float32)[:, None]
    inner = lax.map(walsh, flipped.reshape(N_GRP, N_DEV * ROWS_DEV, COLUMNS))
    column = jnp.arange(N_DEV, dtype=jnp.int32)[None, :, None]
    position = (column * ROWS_DEV + source_row).astype(jnp.int32)
    picked_group = source_group[..., 0]
    total = jnp.zeros((N_GRP, N_DEV, N_DEV * PICKS_PER, COLUMNS), jnp.float32)
    for other in range(N_GRP):
        parity = bit_parity(picked_group & other, N_GRP.bit_length())
        factor = (1 - 2 * parity).astype(jnp.float32)
        total = total + factor[..., None] * inner[other][position]
    sampled = total * (1.0 / math.sqrt(PANEL_ROWS))
    sketch = sampled.reshape(N_GRP, N_DEV, N_DEV, PICKS_PER, COLUMNS).transpose(0, 2, 1, 3, 4).reshape(SKETCH_ROWS, COLUMNS)
    gram = jnp.dot(sketch.T.astype(jnp.float32), sketch.astype(jnp.float32), precision=lax.Precision.HIGHEST, preferred_element_type=jnp.float32) / SKETCH_ROWS
    gram = gram + 0.001 * jnp.eye(COLUMNS, dtype=jnp.float32)
    lower = jnp.linalg.cholesky(gram)
    conditioned = lax.linalg.triangular_solve(lower, panel, left_side=False, lower=True, transpose_a=True)
    return (sketch, conditioned)
```

```python
import functools
import math
import jax
import jax.numpy as jnp
from jax import lax
from jax.experimental import pallas as pl
from jax.experimental.pallas import tpu as pltpu
from jax.sharding import PartitionSpec as P

BLOCK = 128


def pivot_block(tiles):
    count = len(tiles)
    lane = lax.broadcasted_iota(jnp.int32, (8, BLOCK), 1)
    sub = lax.broadcasted_iota(jnp.int32, (8, BLOCK), 0)
    tiles = list(tiles)
    for p in range(count):
        base = 8 * p
        inside = (lane >= base) & (lane < base + 8)
        cols = {
            q: [jnp.broadcast_to(tiles[q][:, base + t : base + t + 1], (8, BLOCK)) for t in range(8)]
            for q in range(p, count)
        }
        tiles[p] = jnp.where(inside, (lane - base == sub).astype(jnp.float32), tiles[p])
        for q in range(p + 1, count):
            tiles[q] = jnp.where(inside, 0.0, tiles[q])
        diag = jnp.ones((8, BLOCK), jnp.float32)
        for t in range(8):
            pivot = jnp.broadcast_to(cols[p][t][t : t + 1, :], (8, BLOCK))
            diag = jnp.where(sub == t, pivot, diag)
            inverse = 1.0 / pivot
            row = jnp.broadcast_to(tiles[p][t : t + 1, :], (8, BLOCK)) * inverse
            heads = [
                jnp.broadcast_to(cols[p][u][t : t + 1, :], (8, BLOCK)) * inverse for u in range(t + 1, 8)
            ]
            for q in range(p, count):
                coef = cols[q][t]
                if q == p:
                    coef = jnp.where(sub > t, coef, 0.0)
                for place, u in enumerate(range(t + 1, 8)):
                    cols[q][u] = cols[q][u] - coef * heads[place]
                tiles[q] = tiles[q] - coef * row
        tiles[p] = tiles[p] * lax.rsqrt(diag)
    return tiles


def matmul(a, b, dims):
    return lax.dot_general(
        a, b, (dims, ((), ())), precision=lax.Precision.HIGHEST, preferred_element_type=jnp.float32
    )


def inverse_factor(work):
    size = work.shape[0]
    rowi = lax.broadcasted_iota(jnp.int32, (BLOCK, BLOCK), 0)
    coli = lax.broadcasted_iota(jnp.int32, (BLOCK, BLOCK), 1)
    wide = lax.broadcasted_iota(jnp.int32, (BLOCK, size), 1)

    def step(k, carry):
        start = pl.multiple_of(k * BLOCK, BLOCK)
        here = pl.ds(start, BLOCK)
        tiles = [
            work[pl.ds(pl.multiple_of(start + 8 * p, 8), 8), here] for p in range(BLOCK // 8)
        ]
        tiles = pivot_block(tiles)
        own = jnp.where(rowi >= coli, jnp.concatenate(tiles, axis=0), 0.0)
        rows = matmul(own, work[here, :], ((1,), (0,)))
        work[here, :] = rows
        work[here, here] = own
        rows = work[here, :]
        work[:, here] = jnp.where(
            lax.broadcasted_iota(jnp.int32, (size, BLOCK), 0) >= start + BLOCK, 0.0, work[:, here]
        )
        left = jnp.where(wide >= start + BLOCK, rows, 0.0)
        work[...] = work[...] - matmul(left, rows, ((0,), (0,)))
        work[here, :] = jnp.where(wide < start + BLOCK, rows, 0.0)
        return carry

    lax.fori_loop(0, size // BLOCK, step, 0)


def add_ridge(gram, sketch_total):
    size = gram.shape[0]
    rowi = lax.broadcasted_iota(jnp.int32, (size, size), 0)
    coli = lax.broadcasted_iota(jnp.int32, (size, size), 1)
    return gram / sketch_total + jnp.where(rowi == coli, 0.001, 0.0)


def gram_kernel(sketch_total, sketch_ref, out_ref, work):
    sketch = sketch_ref[...]
    work[...] = add_ridge(matmul(sketch, sketch, ((0,), (0,))), sketch_total)
    inverse_factor(work)
    out_ref[...] = work[...]


def from_gram_kernel(sketch_total, gram_ref, out_ref, work):
    work[...] = add_ridge(gram_ref[...], sketch_total)
    inverse_factor(work)
    out_ref[...] = work[...]


def bit_parity(value, bits):
    total = jnp.zeros_like(value)
    for bit_place in range(bits):
        total = total + (value >> bit_place & 1)
    return total & 1


def sylvester(order):
    index = jnp.arange(order, dtype=jnp.int32)
    parity = bit_parity(index[:, None] & index[None, :], order.bit_length())
    return (1 - 2 * parity).astype(jnp.float32)


def on_device(panel, signs, source_group, source_row):
    rows_here = panel.shape[0]
    columns = panel.shape[1]
    groups = lax.axis_size("grp")
    devices = lax.axis_size("dev")
    group_here = lax.axis_index("grp")
    highest = lax.Precision.HIGHEST
    flipped = panel * (1 - 2 * signs).astype(jnp.float32)[:, None]
    local = jnp.dot(
        sylvester(rows_here), flipped, precision=highest, preferred_element_type=jnp.float32
    )
    dev_table = sylvester(devices)
    mixed = jnp.einsum(
        "ed,dbc->ebc",
        dev_table,
        lax.all_to_all(
            local.reshape(devices, rows_here // devices, columns),
            "dev",
            split_axis=0,
            concat_axis=0,
            tiled=True,
        ),
        precision=highest,
    )
    inner = mixed
    inner = inner.reshape(rows_here, columns)
    chosen_group = source_group[:, 0, :, 0]
    chosen_row = source_row[:, 0, :]
    width = chosen_group.shape[1]
    per_owner = width // devices
    band_size = rows_here // devices
    dev_here = lax.axis_index("dev")
    stacked = jnp.stack([chosen_group, chosen_row]).reshape(2, groups, devices, per_owner)
    lists = lax.all_to_all(stacked, "dev", split_axis=2, concat_axis=2, tiled=True)
    band_group = lists[0].reshape(-1)
    band_row = lists[1].reshape(-1)
    flat_place = jnp.arange(groups * devices * per_owner, dtype=jnp.int32)
    source_dev = flat_place // per_owner % devices
    flat_index = source_dev * band_size + band_row - dev_here * band_size
    parity = bit_parity(band_group & group_here, groups.bit_length())
    factor = (1 - 2 * parity).astype(jnp.float32)
    gathered = lax.psum_scatter(
        inner[flat_index] * factor[:, None], "grp", scatter_dimension=0, tiled=True
    )
    panel_total = rows_here * devices * groups
    sketch = gathered * (1.0 / math.sqrt(panel_total))
    sketch_total = sketch.shape[0] * devices * groups
    if sketch_total <= rows_here:
        pieces = lax.all_gather(sketch, ("grp", "dev"), axis=0, tiled=True)
        kernel = functools.partial(gram_kernel, sketch_total)
    else:
        partial_gram = jnp.dot(sketch.T, sketch, precision=highest, preferred_element_type=jnp.float32)
        pieces = lax.psum(partial_gram, ("grp", "dev"))
        kernel = functools.partial(from_gram_kernel, sketch_total)
    inverse = pl.pallas_call(
        kernel,
        out_shape=jax.ShapeDtypeStruct((columns, columns), jnp.float32),
        in_specs=[pl.BlockSpec(memory_space=pltpu.VMEM)],
        out_specs=pl.BlockSpec(memory_space=pltpu.VMEM),
        scratch_shapes=[pltpu.VMEM((columns, columns), jnp.float32)],
        name="factor",
    )(pieces)
    conditioned = lax.dot_general(
        panel, inverse, (((1,), (1,)), ((), ())), precision=highest, preferred_element_type=jnp.float32
    )
    return (sketch, conditioned)


def solution(mesh):
    return jax.shard_map(
        on_device,
        mesh=mesh,
        in_specs=(
            P(("grp", "dev"), None),
            P(("grp", "dev")),
            P(None, "dev", None, None),
            P(None, "dev", None),
        ),
        out_specs=(P(("grp", "dev"), None), P(("grp", "dev"), None)),
        check_vma=False,
    )
```

```python
import functools
import math
import jax
import jax.numpy as jnp
from jax import lax
from jax.experimental import pallas as pl
from jax.experimental.pallas import tpu as pltpu
from jax.sharding import PartitionSpec as P

BLOCK = 128


def pivot_block(tiles):
    count = len(tiles)
    lane = lax.broadcasted_iota(jnp.int32, (8, BLOCK), 1)
    sub = lax.broadcasted_iota(jnp.int32, (8, BLOCK), 0)
    tiles = list(tiles)
    for p in range(count):
        base = 8 * p
        inside = (lane >= base) & (lane < base + 8)
        cols = {
            q: [jnp.broadcast_to(tiles[q][:, base + t : base + t + 1], (8, BLOCK)) for t in range(8)]
            for q in range(p, count)
        }
        tiles[p] = jnp.where(inside, (lane - base == sub).astype(jnp.float32), tiles[p])
        for q in range(p + 1, count):
            tiles[q] = jnp.where(inside, 0.0, tiles[q])
        diag = jnp.ones((8, BLOCK), jnp.float32)
        for t in range(8):
            pivot = jnp.broadcast_to(cols[p][t][t : t + 1, :], (8, BLOCK))
            diag = jnp.where(sub == t, pivot, diag)
            inverse = 1.0 / pivot
            row = jnp.broadcast_to(tiles[p][t : t + 1, :], (8, BLOCK)) * inverse
            heads = [
                jnp.broadcast_to(cols[p][u][t : t + 1, :], (8, BLOCK)) * inverse for u in range(t + 1, 8)
            ]
            for q in range(p, count):
                coef = cols[q][t]
                if q == p:
                    coef = jnp.where(sub > t, coef, 0.0)
                for place, u in enumerate(range(t + 1, 8)):
                    cols[q][u] = cols[q][u] - coef * heads[place]
                tiles[q] = tiles[q] - coef * row
        tiles[p] = tiles[p] * lax.rsqrt(diag)
    return tiles


def matmul(a, b, dims):
    return lax.dot_general(
        a, b, (dims, ((), ())), precision=lax.Precision.HIGHEST, preferred_element_type=jnp.float32
    )


def inverse_factor(work):
    size = work.shape[0]
    rowi = lax.broadcasted_iota(jnp.int32, (BLOCK, BLOCK), 0)
    coli = lax.broadcasted_iota(jnp.int32, (BLOCK, BLOCK), 1)
    wide = lax.broadcasted_iota(jnp.int32, (BLOCK, size), 1)

    def step(k, carry):
        start = pl.multiple_of(k * BLOCK, BLOCK)
        here = pl.ds(start, BLOCK)
        tiles = [
            work[pl.ds(pl.multiple_of(start + 8 * p, 8), 8), here] for p in range(BLOCK // 8)
        ]
        tiles = pivot_block(tiles)
        own = jnp.where(rowi >= coli, jnp.concatenate(tiles, axis=0), 0.0)
        rows = matmul(own, work[here, :], ((1,), (0,)))
        work[here, :] = rows
        work[here, here] = own
        rows = work[here, :]
        work[:, here] = jnp.where(
            lax.broadcasted_iota(jnp.int32, (size, BLOCK), 0) >= start + BLOCK, 0.0, work[:, here]
        )
        left = jnp.where(wide >= start + BLOCK, rows, 0.0)
        work[...] = work[...] - matmul(left, rows, ((0,), (0,)))
        work[here, :] = jnp.where(wide < start + BLOCK, rows, 0.0)
        return carry

    lax.fori_loop(0, size // BLOCK, step, 0)


def add_ridge(gram, sketch_total):
    size = gram.shape[0]
    rowi = lax.broadcasted_iota(jnp.int32, (size, size), 0)
    coli = lax.broadcasted_iota(jnp.int32, (size, size), 1)
    return gram / sketch_total + jnp.where(rowi == coli, 0.001, 0.0)


def gram_kernel(sketch_total, sketch_ref, out_ref, work):
    sketch = sketch_ref[...]
    work[...] = add_ridge(matmul(sketch, sketch, ((0,), (0,))), sketch_total)
    inverse_factor(work)
    out_ref[...] = work[...]


def from_gram_kernel(sketch_total, gram_ref, out_ref, work):
    work[...] = add_ridge(gram_ref[...], sketch_total)
    inverse_factor(work)
    out_ref[...] = work[...]


def flip(index, mask):
    bit = 1
    while bit <= mask:
        if mask & bit:
            index = index + bit - 2 * bit * lax.rem(lax.div(index, bit), 2)
        bit = 2 * bit
    return index


def parity_sign(value, bits):
    span = 1
    while span < bits:
        span = span * 2
    while span > 1:
        span = span // 2
        value = value ^ (value >> span)
    return (1 - 2 * (value & 1)).astype(jnp.float32)


def sketch_kernel(
    groups, per_owner, scale, panel_ref, signs_ref, picks_ref, whole_ref, own_ref,
    lists, high, low, choice, acc, from_core, from_first, from_second, from_group, send, recv,
):
    devices = 8
    rows_here, columns = panel_ref.shape
    half = columns // 2
    left, right = pl.ds(0, half), pl.ds(half, half)
    band = groups * devices * per_owner
    share = devices * per_owner
    me = lax.axis_index("dev")
    here = lax.axis_index("grp")

    barrier = pltpu.get_barrier_semaphore()
    for mask in range(1, devices):
        pl.semaphore_signal(
            barrier, inc=1, device_id={"dev": flip(me, mask)}, device_id_type=pl.DeviceIdType.MESH
        )
    for mask in range(1, groups):
        pl.semaphore_signal(
            barrier, inc=1, device_id={"grp": flip(here, mask)}, device_id_type=pl.DeviceIdType.MESH
        )
    pl.semaphore_wait(barrier, devices + groups - 2)

    taken = []

    def transfer(source, target, axis, mask):
        place = len(taken)
        taken.append(place)
        peer = flip(me if axis == "dev" else here, mask)
        copy = pltpu.make_async_remote_copy(
            src_ref=source,
            dst_ref=target,
            send_sem=send.at[place],
            recv_sem=recv.at[place],
            device_id={axis: peer},
            device_id_type=pl.DeviceIdType.MESH,
        )
        copy.start()
        return copy

    sends = []
    listed = [transfer(picks_ref, lists.at[mask], "dev", mask) for mask in range(1, devices)]
    flipped = panel_ref[...] * (1 - 2 * signs_ref[...]).astype(jnp.float32)
    top = flipped.astype(jnp.bfloat16)
    high[...] = top
    low[...] = (flipped - top.astype(jnp.float32)).astype(jnp.bfloat16)
    lists[0] = picks_ref[...]
    for copy in listed:
        copy.wait_recv()
    sends += listed

    slot = lax.broadcasted_iota(jnp.int32, (devices, band), 0)
    group_of = jnp.concatenate([lists[m][0:1, :] for m in range(devices)], axis=0)
    row_of = jnp.concatenate([lists[m][1:2, :] for m in range(devices)], axis=0)
    value = (group_of * devices + (slot ^ me)) * rows_here + row_of
    total = devices * band
    place = lax.broadcasted_iota(jnp.int32, (total, band), 0)
    entry = lax.broadcasted_iota(jnp.int32, (total, band), 1)
    owner = (place // band) ^ me
    group = ((place // share) % groups) ^ here
    wanted = group * share + owner * per_owner + place % per_owner
    spread = lax.dot_general(
        (entry == wanted).astype(jnp.float32),
        value.astype(jnp.float32),
        (((1,), (1,)), ((), ())),
        precision=lax.Precision.HIGHEST,
        preferred_element_type=jnp.float32,
    )
    place = lax.broadcasted_iota(jnp.int32, (total, devices), 0)
    held = lax.broadcasted_iota(jnp.int32, (total, devices), 1)
    source = ((place // per_owner) % devices) ^ me
    choice[...] = jnp.sum(jnp.where(held == source, spread, 0.0), axis=1, keepdims=True).astype(jnp.int32)

    def mixed(chunk):
        pick = jnp.broadcast_to(choice[chunk * band : (chunk + 1) * band, :], (band, 128))
        lane = lax.broadcasted_iota(jnp.int32, (band, 128), 1)
        rank = here * devices + me
        above = parity_sign((pick // rows_here) & rank, (groups * devices).bit_length() - 1)
        table = [parity_sign(pick & lane, 7) * above]
        bit = 7
        while 128 * len(table) < rows_here:
            turn = (1 - 2 * ((pick >> bit) & 1)).astype(jnp.float32)
            table = table + [part * turn for part in table]
            bit = bit + 1
        table = jnp.concatenate([part.astype(jnp.bfloat16) for part in table], axis=1)
        dims = (((1,), (0,)), ((), ()))
        return lax.dot_general(
            table, high[...], dims, preferred_element_type=jnp.float32
        ) + lax.dot_general(table, low[...], dims, preferred_element_type=jnp.float32)

    core = {}
    for chunk in (7, 3, 5, 1):
        acc[chunk] = mixed(chunk)
        core[chunk - 1] = transfer(acc.at[chunk], from_core.at[chunk // 2], "dev", 1)
    first, second = {}, {}
    for chunk in (6, 2, 4, 0):
        acc[chunk] = mixed(chunk)
        core[chunk].wait_recv()
        acc[chunk] = acc[chunk] + from_core[chunk // 2]
        if chunk & 2:
            first["left", chunk - 2] = transfer(
                acc.at[chunk, :, left], from_first.at[chunk // 4, :, left], "dev", 2
            )
        if chunk & 4:
            first["right", chunk - 4] = transfer(
                acc.at[chunk, :, right], from_first.at[(chunk & 2) // 2, :, right], "dev", 4
            )
    first["left", 4].wait_recv()
    acc[4, :, left] = acc[4, :, left] + from_first[1, :, left]
    second["left"] = transfer(acc.at[4, :, left], from_second.at[:, left], "dev", 4)
    first["right", 2].wait_recv()
    acc[2, :, right] = acc[2, :, right] + from_first[1, :, right]
    second["right"] = transfer(acc.at[2, :, right], from_second.at[:, right], "dev", 2)
    first["left", 0].wait_recv()
    first["right", 0].wait_recv()
    acc[0] = acc[0] + from_first[0]
    second["left"].wait_recv()
    second["right"].wait_recv()
    acc[0] = acc[0] + from_second[...]
    sends += list(core.values()) + list(first.values()) + list(second.values())
    across = [
        transfer(acc.at[0, pl.ds(block * share, share)], from_group.at[block], "grp", block)
        for block in range(1, groups)
    ]
    result = acc[0, 0:share, :]
    for block in range(1, groups):
        across[block - 1].wait_recv()
        result = result + from_group[block]
    sends += across
    result = result * scale
    own_ref[...] = result
    whole_ref[0, 0:share, :] = result

    across = [
        transfer(
            whole_ref.at[0, pl.ds(0, share)], whole_ref.at[0, pl.ds(block * share, share)], "grp", block
        )
        for block in range(1, groups)
    ]
    for copy in across:
        copy.wait_recv()
    sends += across
    out = [
        transfer(whole_ref.at[0, :, left], whole_ref.at[4, :, left], "dev", 4),
        transfer(whole_ref.at[0, :, right], whole_ref.at[2, :, right], "dev", 2),
        transfer(whole_ref.at[0, :, left], whole_ref.at[2, :, left], "dev", 2),
        transfer(whole_ref.at[0, :, right], whole_ref.at[4, :, right], "dev", 4),
    ]
    last = [transfer(whole_ref.at[0], whole_ref.at[1], "dev", 1)]
    out[0].wait_recv()
    relay = [transfer(whole_ref.at[4, :, left], whole_ref.at[6, :, left], "dev", 2)]
    out[1].wait_recv()
    relay.append(transfer(whole_ref.at[2, :, right], whole_ref.at[6, :, right], "dev", 4))
    out[2].wait_recv()
    last.append(transfer(whole_ref.at[2], whole_ref.at[3], "dev", 1))
    out[3].wait_recv()
    last.append(transfer(whole_ref.at[4], whole_ref.at[5], "dev", 1))
    relay[0].wait_recv()
    relay[1].wait_recv()
    last.append(transfer(whole_ref.at[6], whole_ref.at[7], "dev", 1))
    for copy in last:
        copy.wait_recv()
    sends += out + relay + last
    for copy in sends:
        copy.wait_send()


def kernel_sketch(panel, signs, source_group, source_row, groups, devices):
    rows_here, columns = panel.shape
    per_owner = source_row.shape[2] // devices
    band = groups * devices * per_owner
    share = devices * per_owner
    picks = jnp.stack([source_group.reshape(band), source_row.reshape(band)])
    picks = jnp.concatenate([picks, jnp.zeros((6, band), jnp.int32)], axis=0)
    scale = 1.0 / math.sqrt(rows_here * devices * groups)
    vmem = pl.BlockSpec(memory_space=pltpu.VMEM)
    f32 = jnp.float32
    whole, own = pl.pallas_call(
        functools.partial(sketch_kernel, groups, per_owner, scale),
        out_shape=(
            jax.ShapeDtypeStruct((devices, band, columns), f32),
            jax.ShapeDtypeStruct((share, columns), f32),
        ),
        in_specs=[vmem] * 3,
        out_specs=(vmem, vmem),
        scratch_shapes=[
            pltpu.VMEM((devices, 8, band), jnp.int32),
            pltpu.VMEM((rows_here, columns), jnp.bfloat16),
            pltpu.VMEM((rows_here, columns), jnp.bfloat16),
            pltpu.VMEM((devices * band, 1), jnp.int32),
            pltpu.VMEM((devices, band, columns), f32),
            pltpu.VMEM((devices // 2, band, columns), f32),
            pltpu.VMEM((2, band, columns), f32),
            pltpu.VMEM((band, columns), f32),
            pltpu.VMEM((groups, share, columns), f32),
            pltpu.SemaphoreType.DMA((40,)),
            pltpu.SemaphoreType.DMA((40,)),
        ],
        compiler_params=pltpu.CompilerParams(collective_id=0, has_side_effects=True),
        name="sketch",
    )(panel, signs[:, None], picks)
    return whole.reshape(devices * band, columns), own


def bit_parity(value, bits):
    total = jnp.zeros_like(value)
    for bit_place in range(bits):
        total = total + (value >> bit_place & 1)
    return total & 1


def sylvester(order):
    index = jnp.arange(order, dtype=jnp.int32)
    parity = bit_parity(index[:, None] & index[None, :], order.bit_length())
    return (1 - 2 * parity).astype(jnp.float32)


def general_sketch(panel, signs, source_group, source_row):
    rows_here = panel.shape[0]
    columns = panel.shape[1]
    groups = lax.axis_size("grp")
    devices = lax.axis_size("dev")
    group_here = lax.axis_index("grp")
    highest = lax.Precision.HIGHEST
    flipped = panel * (1 - 2 * signs).astype(jnp.float32)[:, None]
    local = jnp.dot(
        sylvester(rows_here), flipped, precision=highest, preferred_element_type=jnp.float32
    )
    dev_table = sylvester(devices)
    mixed = jnp.einsum(
        "ed,dbc->ebc",
        dev_table,
        lax.all_to_all(
            local.reshape(devices, rows_here // devices, columns),
            "dev",
            split_axis=0,
            concat_axis=0,
            tiled=True,
        ),
        precision=highest,
    )
    inner = mixed
    inner = inner.reshape(rows_here, columns)
    chosen_group = source_group[:, 0, :, 0]
    chosen_row = source_row[:, 0, :]
    width = chosen_group.shape[1]
    per_owner = width // devices
    band_size = rows_here // devices
    dev_here = lax.axis_index("dev")
    stacked = jnp.stack([chosen_group, chosen_row]).reshape(2, groups, devices, per_owner)
    lists = lax.all_to_all(stacked, "dev", split_axis=2, concat_axis=2, tiled=True)
    band_group = lists[0].reshape(-1)
    band_row = lists[1].reshape(-1)
    flat_place = jnp.arange(groups * devices * per_owner, dtype=jnp.int32)
    source_dev = flat_place // per_owner % devices
    flat_index = source_dev * band_size + band_row - dev_here * band_size
    parity = bit_parity(band_group & group_here, groups.bit_length())
    factor = (1 - 2 * parity).astype(jnp.float32)
    gathered = lax.psum_scatter(
        inner[flat_index] * factor[:, None], "grp", scatter_dimension=0, tiled=True
    )
    panel_total = rows_here * devices * groups
    sketch = gathered * (1.0 / math.sqrt(panel_total))
    sketch_total = sketch.shape[0] * devices * groups
    partial_gram = jnp.dot(sketch.T, sketch, precision=highest, preferred_element_type=jnp.float32)
    return sketch, lax.psum(partial_gram, ("grp", "dev"))


def on_device(panel, signs, source_group, source_row):
    rows_here, columns = panel.shape
    groups = lax.axis_size("grp")
    devices = lax.axis_size("dev")
    highest = lax.Precision.HIGHEST
    width = source_row.shape[2]
    sketch_total = groups * devices * width
    fits = groups & (groups - 1) == 0 and groups * width == 128 and rows_here % 128 == 0
    if devices == 8 and fits and rows_here & (rows_here - 1) == 0:
        pieces, sketch = kernel_sketch(panel, signs, source_group, source_row, groups, devices)
        kernel = functools.partial(gram_kernel, sketch_total)
    else:
        sketch, pieces = general_sketch(panel, signs, source_group, source_row)
        kernel = functools.partial(from_gram_kernel, sketch_total)
    inverse = pl.pallas_call(
        kernel,
        out_shape=jax.ShapeDtypeStruct((columns, columns), jnp.float32),
        in_specs=[pl.BlockSpec(memory_space=pltpu.VMEM)],
        out_specs=pl.BlockSpec(memory_space=pltpu.VMEM),
        scratch_shapes=[pltpu.VMEM((columns, columns), jnp.float32)],
        name="factor",
    )(pieces)
    conditioned = lax.dot_general(
        panel, inverse, (((1,), (1,)), ((), ())), precision=highest, preferred_element_type=jnp.float32
    )
    return (sketch, conditioned)


def solution(mesh):
    return jax.shard_map(
        on_device,
        mesh=mesh,
        in_specs=(
            P(("grp", "dev"), None),
            P(("grp", "dev")),
            P(None, "dev", None, None),
            P(None, "dev", None),
        ),
        out_specs=(P(("grp", "dev"), None), P(("grp", "dev"), None)),
        check_vma=False,
    )
```

```python
import functools
import math
import jax
import jax.numpy as jnp
from jax import lax
from jax.experimental import pallas as pl
from jax.experimental.pallas import tpu as pltpu
from jax.sharding import PartitionSpec as P

BLOCK = 128


def pivot_block(tiles):
    count = len(tiles)
    lane = lax.broadcasted_iota(jnp.int32, (8, BLOCK), 1)
    sub = lax.broadcasted_iota(jnp.int32, (8, BLOCK), 0)
    tiles = list(tiles)
    for p in range(count):
        base = 8 * p
        inside = (lane >= base) & (lane < base + 8)
        cols = {
            q: [jnp.broadcast_to(tiles[q][:, base + t : base + t + 1], (8, BLOCK)) for t in range(8)]
            for q in range(p, count)
        }
        tiles[p] = jnp.where(inside, (lane - base == sub).astype(jnp.float32), tiles[p])
        for q in range(p + 1, count):
            tiles[q] = jnp.where(inside, 0.0, tiles[q])
        diag = jnp.ones((8, BLOCK), jnp.float32)
        for t in range(8):
            pivot = jnp.broadcast_to(cols[p][t][t : t + 1, :], (8, BLOCK))
            diag = jnp.where(sub == t, pivot, diag)
            inverse = 1.0 / pivot
            row = jnp.broadcast_to(tiles[p][t : t + 1, :], (8, BLOCK)) * inverse
            heads = [
                jnp.broadcast_to(cols[p][u][t : t + 1, :], (8, BLOCK)) * inverse for u in range(t + 1, 8)
            ]
            for q in range(p, count):
                coef = cols[q][t]
                if q == p:
                    coef = jnp.where(sub > t, coef, 0.0)
                for place, u in enumerate(range(t + 1, 8)):
                    cols[q][u] = cols[q][u] - coef * heads[place]
                tiles[q] = tiles[q] - coef * row
        tiles[p] = tiles[p] * lax.rsqrt(diag)
    return tiles


def matmul(a, b, dims):
    return lax.dot_general(
        a, b, (dims, ((), ())), precision=lax.Precision.HIGHEST, preferred_element_type=jnp.float32
    )


def inverse_factor(work):
    size = work.shape[0]
    rowi = lax.broadcasted_iota(jnp.int32, (BLOCK, BLOCK), 0)
    coli = lax.broadcasted_iota(jnp.int32, (BLOCK, BLOCK), 1)
    wide = lax.broadcasted_iota(jnp.int32, (BLOCK, size), 1)

    def step(k, carry):
        start = pl.multiple_of(k * BLOCK, BLOCK)
        here = pl.ds(start, BLOCK)
        tiles = [
            work[pl.ds(pl.multiple_of(start + 8 * p, 8), 8), here] for p in range(BLOCK // 8)
        ]
        tiles = pivot_block(tiles)
        own = jnp.where(rowi >= coli, jnp.concatenate(tiles, axis=0), 0.0)
        rows = matmul(own, work[here, :], ((1,), (0,)))
        work[here, :] = rows
        work[here, here] = own
        rows = work[here, :]
        work[:, here] = jnp.where(
            lax.broadcasted_iota(jnp.int32, (size, BLOCK), 0) >= start + BLOCK, 0.0, work[:, here]
        )
        left = jnp.where(wide >= start + BLOCK, rows, 0.0)
        work[...] = work[...] - matmul(left, rows, ((0,), (0,)))
        work[here, :] = jnp.where(wide < start + BLOCK, rows, 0.0)
        return carry

    lax.fori_loop(0, size // BLOCK, step, 0)


def add_ridge(gram, sketch_total):
    size = gram.shape[0]
    rowi = lax.broadcasted_iota(jnp.int32, (size, size), 0)
    coli = lax.broadcasted_iota(jnp.int32, (size, size), 1)
    return gram / sketch_total + jnp.where(rowi == coli, 0.001, 0.0)


def halves(value):
    high = value.astype(jnp.bfloat16)
    return high, (value - high.astype(jnp.float32)).astype(jnp.bfloat16)


def split_matmul(a, b, dims):
    dot = functools.partial(
        lax.dot_general, dimension_numbers=(dims, ((), ())), preferred_element_type=jnp.float32
    )
    return dot(a[0], b[0]) + (dot(a[0], b[1]) + dot(a[1], b[0]))


def finish(work, panel_ref, out_ref):
    rows, columns = panel_ref.shape
    part = columns // 2
    for base in (0, part):
        deep = base + part
        factor = halves(work[base : base + part, 0:deep])
        out_ref[:, base : base + part] = split_matmul(
            halves(panel_ref[:, 0:deep]), factor, ((1,), (1,))
        )


def gram_kernel(sketch_total, sketch_ref, panel_ref, own_ref, out_ref, work):
    own_ref[...] = sketch_ref[0 : own_ref.shape[0], :]
    sketch = halves(sketch_ref[...])
    work[...] = add_ridge(split_matmul(sketch, sketch, ((0,), (0,))), sketch_total)
    inverse_factor(work)
    finish(work, panel_ref, out_ref)


def from_gram_kernel(sketch_total, gram_ref, panel_ref, out_ref, work):
    work[...] = add_ridge(gram_ref[...], sketch_total)
    inverse_factor(work)
    finish(work, panel_ref, out_ref)


def flip(index, mask):
    bit = 1
    while bit <= mask:
        if mask & bit:
            index = index + bit - 2 * bit * lax.rem(lax.div(index, bit), 2)
        bit = 2 * bit
    return index


def parity_sign(value, bits):
    span = 1
    while span < bits:
        span = span * 2
    while span > 1:
        span = span // 2
        value = value ^ (value >> span)
    return (1 - 2 * (value & 1)).astype(jnp.float32)


def sketch_kernel(
    groups, per_owner, scale, panel_ref, signs_ref, group_ref, row_ref, whole_ref,
    lists, values, high, low, choice, acc, from_core, from_first, from_second, from_group, send, recv,
):
    devices = 8
    rows_here, columns = panel_ref.shape
    half = columns // 2
    left, right = pl.ds(0, half), pl.ds(half, half)
    band = groups * devices * per_owner
    share = devices * per_owner
    me = lax.axis_index("dev")
    here = lax.axis_index("grp")

    barrier = pltpu.get_barrier_semaphore()
    for mask in range(1, devices):
        pl.semaphore_signal(
            barrier, inc=1, device_id={"dev": flip(me, mask)}, device_id_type=pl.DeviceIdType.MESH
        )
    for mask in range(1, groups):
        pl.semaphore_signal(
            barrier, inc=1, device_id={"grp": flip(here, mask)}, device_id_type=pl.DeviceIdType.MESH
        )
    pl.semaphore_wait(barrier, devices + groups - 2)

    taken = []

    def transfer(source, target, axis, mask):
        place = len(taken)
        taken.append(place)
        peer = flip(me if axis == "dev" else here, mask)
        copy = pltpu.make_async_remote_copy(
            src_ref=source,
            dst_ref=target,
            send_sem=send.at[place],
            recv_sem=recv.at[place],
            device_id={axis: peer},
            device_id_type=pl.DeviceIdType.MESH,
        )
        copy.start()
        return copy

    sends = []
    listed = [transfer(group_ref, lists.at[0, mask], "dev", mask) for mask in range(1, devices)]
    listed += [transfer(row_ref, lists.at[1, mask], "dev", mask) for mask in range(1, devices)]
    top = panel_ref[...].astype(jnp.bfloat16)
    high[...] = top
    low[...] = (panel_ref[...] - top.astype(jnp.float32)).astype(jnp.bfloat16)
    lists[0, 0] = group_ref[...]
    lists[1, 0] = row_ref[...]
    for copy in listed:
        copy.wait_recv()
    sends += listed

    for slot in range(devices):
        values[slot * groups : (slot + 1) * groups, :] = (
            lists[0, slot] * devices + flip(me, slot)
        ) * rows_here + lists[1, slot]
    total = devices * band
    width = devices * per_owner
    place = lax.broadcasted_iota(jnp.int32, (total, width), 0)
    entry = lax.broadcasted_iota(jnp.int32, (total, width), 1)
    wanted = ((place // band) ^ me) * per_owner + place % per_owner
    spread = lax.dot_general(
        (entry == wanted).astype(jnp.float32),
        values[...].astype(jnp.float32),
        (((1,), (1,)), ((), ())),
        precision=lax.Precision.HIGHEST,
        preferred_element_type=jnp.float32,
    )
    place = lax.broadcasted_iota(jnp.int32, (total, devices * groups), 0)
    held = lax.broadcasted_iota(jnp.int32, (total, devices * groups), 1)
    source = (((place // per_owner) % devices) ^ me) * groups + (((place // share) % groups) ^ here)
    choice[...] = jnp.sum(jnp.where(held == source, spread, 0.0), axis=1, keepdims=True).astype(jnp.int32)

    def mixed(chunk):
        pick = jnp.broadcast_to(choice[chunk * band : (chunk + 1) * band, :], (band, 128))
        lane = lax.broadcasted_iota(jnp.int32, (band, 128), 1)
        rank = here * devices + me
        above = parity_sign((pick // rows_here) & rank, (groups * devices).bit_length() - 1)
        table = [parity_sign(pick & lane, 7) * above]
        bit = 7
        while 128 * len(table) < rows_here:
            turn = (1 - 2 * ((pick >> bit) & 1)).astype(jnp.float32)
            table = table + [part * turn for part in table]
            bit = bit + 1
        turns = (1 - 2 * signs_ref[...]).astype(jnp.float32)
        table = [part * turns[i : i + 1, :] for i, part in enumerate(table)]
        table = jnp.concatenate([part.astype(jnp.bfloat16) for part in table], axis=1)
        dims = (((1,), (0,)), ((), ()))
        return lax.dot_general(
            table, high[...], dims, preferred_element_type=jnp.float32
        ) + lax.dot_general(table, low[...], dims, preferred_element_type=jnp.float32)

    core = {}
    for chunk in (7, 3, 5, 1):
        acc[chunk] = mixed(chunk)
        core[chunk - 1] = transfer(acc.at[chunk], from_core.at[chunk // 2], "dev", 1)
    first, second = {}, {}
    for chunk in (6, 2, 4, 0):
        acc[chunk] = mixed(chunk)
        core[chunk].wait_recv()
        acc[chunk] = acc[chunk] + from_core[chunk // 2]
        if chunk & 2:
            first["left", chunk - 2] = transfer(
                acc.at[chunk, :, left], from_first.at[chunk // 4, :, left], "dev", 2
            )
        if chunk & 4:
            first["right", chunk - 4] = transfer(
                acc.at[chunk, :, right], from_first.at[(chunk & 2) // 2, :, right], "dev", 4
            )
    first["left", 4].wait_recv()
    acc[4, :, left] = acc[4, :, left] + from_first[1, :, left]
    second["left"] = transfer(acc.at[4, :, left], from_second.at[:, left], "dev", 4)
    first["right", 2].wait_recv()
    acc[2, :, right] = acc[2, :, right] + from_first[1, :, right]
    second["right"] = transfer(acc.at[2, :, right], from_second.at[:, right], "dev", 2)
    first["left", 0].wait_recv()
    first["right", 0].wait_recv()
    acc[0] = acc[0] + from_first[0]
    second["left"].wait_recv()
    second["right"].wait_recv()
    acc[0] = acc[0] + from_second[...]
    sends += list(core.values()) + list(first.values()) + list(second.values())
    across = [
        transfer(acc.at[0, pl.ds(block * share, share)], from_group.at[block], "grp", block)
        for block in range(1, groups)
    ]
    result = acc[0, 0:share, :]
    for block in range(1, groups):
        across[block - 1].wait_recv()
        result = result + from_group[block]
    sends += across
    result = result * scale
    whole_ref[0, 0:share, :] = result

    across = [
        transfer(
            whole_ref.at[0, pl.ds(0, share)], whole_ref.at[0, pl.ds(block * share, share)], "grp", block
        )
        for block in range(1, groups)
    ]
    for copy in across:
        copy.wait_recv()
    sends += across
    out = [
        transfer(whole_ref.at[0, :, left], whole_ref.at[4, :, left], "dev", 4),
        transfer(whole_ref.at[0, :, right], whole_ref.at[2, :, right], "dev", 2),
        transfer(whole_ref.at[0, :, left], whole_ref.at[2, :, left], "dev", 2),
        transfer(whole_ref.at[0, :, right], whole_ref.at[4, :, right], "dev", 4),
    ]
    last = [transfer(whole_ref.at[0], whole_ref.at[1], "dev", 1)]
    out[0].wait_recv()
    relay = [transfer(whole_ref.at[4, :, left], whole_ref.at[6, :, left], "dev", 2)]
    out[1].wait_recv()
    relay.append(transfer(whole_ref.at[2, :, right], whole_ref.at[6, :, right], "dev", 4))
    out[2].wait_recv()
    last.append(transfer(whole_ref.at[2], whole_ref.at[3], "dev", 1))
    out[3].wait_recv()
    last.append(transfer(whole_ref.at[4], whole_ref.at[5], "dev", 1))
    relay[0].wait_recv()
    relay[1].wait_recv()
    last.append(transfer(whole_ref.at[6], whole_ref.at[7], "dev", 1))
    for copy in last:
        copy.wait_recv()
    sends += out + relay + last
    for copy in sends:
        copy.wait_send()


def kernel_sketch(panel, signs, source_group, source_row, groups, devices):
    rows_here, columns = panel.shape
    per_owner = source_row.shape[2] // devices
    band = groups * devices * per_owner
    share = devices * per_owner
    scale = 1.0 / math.sqrt(rows_here * devices * groups)
    vmem = pl.BlockSpec(memory_space=pltpu.VMEM)
    f32 = jnp.float32
    whole = pl.pallas_call(
        functools.partial(sketch_kernel, groups, per_owner, scale),
        out_shape=jax.ShapeDtypeStruct((devices, band, columns), f32),
        in_specs=[vmem] * 4,
        out_specs=vmem,
        scratch_shapes=[
            pltpu.VMEM((2, devices, groups, share), jnp.int32),
            pltpu.VMEM((devices * groups, share), jnp.int32),
            pltpu.VMEM((rows_here, columns), jnp.bfloat16),
            pltpu.VMEM((rows_here, columns), jnp.bfloat16),
            pltpu.VMEM((devices * band, 1), jnp.int32),
            pltpu.VMEM((devices, band, columns), f32),
            pltpu.VMEM((devices // 2, band, columns), f32),
            pltpu.VMEM((2, band, columns), f32),
            pltpu.VMEM((band, columns), f32),
            pltpu.VMEM((groups, share, columns), f32),
            pltpu.SemaphoreType.DMA((56,)),
            pltpu.SemaphoreType.DMA((56,)),
        ],
        compiler_params=pltpu.CompilerParams(collective_id=0, has_side_effects=True),
        name="sketch",
    )(
        panel,
        signs.reshape(rows_here // 128, 128),
        source_group.reshape(groups, share),
        source_row.reshape(groups, share),
    )
    return whole.reshape(devices * band, columns)


def bit_parity(value, bits):
    total = jnp.zeros_like(value)
    for bit_place in range(bits):
        total = total + (value >> bit_place & 1)
    return total & 1


def sylvester(order):
    index = jnp.arange(order, dtype=jnp.int32)
    parity = bit_parity(index[:, None] & index[None, :], order.bit_length())
    return (1 - 2 * parity).astype(jnp.float32)


def general_sketch(panel, signs, source_group, source_row):
    rows_here = panel.shape[0]
    columns = panel.shape[1]
    groups = lax.axis_size("grp")
    devices = lax.axis_size("dev")
    group_here = lax.axis_index("grp")
    highest = lax.Precision.HIGHEST
    flipped = panel * (1 - 2 * signs).astype(jnp.float32)[:, None]
    local = jnp.dot(
        sylvester(rows_here), flipped, precision=highest, preferred_element_type=jnp.float32
    )
    dev_table = sylvester(devices)
    mixed = jnp.einsum(
        "ed,dbc->ebc",
        dev_table,
        lax.all_to_all(
            local.reshape(devices, rows_here // devices, columns),
            "dev",
            split_axis=0,
            concat_axis=0,
            tiled=True,
        ),
        precision=highest,
    )
    inner = mixed
    inner = inner.reshape(rows_here, columns)
    chosen_group = source_group[:, 0, :, 0]
    chosen_row = source_row[:, 0, :]
    width = chosen_group.shape[1]
    per_owner = width // devices
    band_size = rows_here // devices
    dev_here = lax.axis_index("dev")
    stacked = jnp.stack([chosen_group, chosen_row]).reshape(2, groups, devices, per_owner)
    lists = lax.all_to_all(stacked, "dev", split_axis=2, concat_axis=2, tiled=True)
    band_group = lists[0].reshape(-1)
    band_row = lists[1].reshape(-1)
    flat_place = jnp.arange(groups * devices * per_owner, dtype=jnp.int32)
    source_dev = flat_place // per_owner % devices
    flat_index = source_dev * band_size + band_row - dev_here * band_size
    parity = bit_parity(band_group & group_here, groups.bit_length())
    factor = (1 - 2 * parity).astype(jnp.float32)
    gathered = lax.psum_scatter(
        inner[flat_index] * factor[:, None], "grp", scatter_dimension=0, tiled=True
    )
    panel_total = rows_here * devices * groups
    sketch = gathered * (1.0 / math.sqrt(panel_total))
    sketch_total = sketch.shape[0] * devices * groups
    partial_gram = jnp.dot(sketch.T, sketch, precision=highest, preferred_element_type=jnp.float32)
    return sketch, lax.psum(partial_gram, ("grp", "dev"))


def on_device(panel, signs, source_group, source_row):
    rows_here, columns = panel.shape
    groups = lax.axis_size("grp")
    devices = lax.axis_size("dev")
    width = source_row.shape[2]
    sketch_total = groups * devices * width
    fits = groups & (groups - 1) == 0 and groups * width == 128 and rows_here % 128 == 0
    if devices == 8 and fits and rows_here & (rows_here - 1) == 0:
        pieces = kernel_sketch(panel, signs, source_group, source_row, groups, devices)
        kernel, shapes = gram_kernel, [(width, columns), (rows_here, columns)]
    else:
        sketch, pieces = general_sketch(panel, signs, source_group, source_row)
        kernel, shapes = from_gram_kernel, [(rows_here, columns)]
    *own, conditioned = pl.pallas_call(
        functools.partial(kernel, sketch_total),
        out_shape=[jax.ShapeDtypeStruct(shape, jnp.float32) for shape in shapes],
        in_specs=[pl.BlockSpec(memory_space=pltpu.VMEM)] * 2,
        out_specs=[pl.BlockSpec(memory_space=pltpu.VMEM)] * len(shapes),
        scratch_shapes=[pltpu.VMEM((columns, columns), jnp.float32)],
        name="factor",
    )(pieces, panel)
    if own:
        sketch = own[0]
    return (sketch, conditioned)


def solution(mesh):
    return jax.shard_map(
        on_device,
        mesh=mesh,
        in_specs=(
            P(("grp", "dev"), None),
            P(("grp", "dev")),
            P(None, "dev", None, None),
            P(None, "dev", None),
        ),
        out_specs=(P(("grp", "dev"), None), P(("grp", "dev"), None)),
        check_vma=False,
    )
```

```python
import functools
import math
import jax
import jax.numpy as jnp
from jax import lax
from jax.experimental import pallas as pl
from jax.experimental.pallas import tpu as pltpu
from jax.sharding import PartitionSpec as P

BLOCK = 128


def pivot_block(tiles):
    count = len(tiles)
    lane = lax.broadcasted_iota(jnp.int32, (8, BLOCK), 1)
    sub = lax.broadcasted_iota(jnp.int32, (8, BLOCK), 0)
    tiles = list(tiles)
    for p in range(count):
        base = 8 * p
        inside = (lane >= base) & (lane < base + 8)
        cols = {
            q: [jnp.broadcast_to(tiles[q][:, base + t : base + t + 1], (8, BLOCK)) for t in range(8)]
            for q in range(p, count)
        }
        tiles[p] = jnp.where(inside, (lane - base == sub).astype(jnp.float32), tiles[p])
        for q in range(p + 1, count):
            tiles[q] = jnp.where(inside, 0.0, tiles[q])
        diag = jnp.ones((8, BLOCK), jnp.float32)
        for t in range(8):
            pivot = jnp.broadcast_to(cols[p][t][t : t + 1, :], (8, BLOCK))
            diag = jnp.where(sub == t, pivot, diag)
            inverse = 1.0 / pivot
            row = jnp.broadcast_to(tiles[p][t : t + 1, :], (8, BLOCK)) * inverse
            heads = [
                jnp.broadcast_to(cols[p][u][t : t + 1, :], (8, BLOCK)) * inverse for u in range(t + 1, 8)
            ]
            for q in range(p, count):
                coef = cols[q][t]
                if q == p:
                    coef = jnp.where(sub > t, coef, 0.0)
                for place, u in enumerate(range(t + 1, 8)):
                    cols[q][u] = cols[q][u] - coef * heads[place]
                tiles[q] = tiles[q] - coef * row
        tiles[p] = tiles[p] * lax.rsqrt(diag)
    return tiles


def matmul(a, b, dims):
    return lax.dot_general(
        a, b, (dims, ((), ())), precision=lax.Precision.HIGHEST, preferred_element_type=jnp.float32
    )


def inverse_factor(work):
    size = work.shape[0]
    rowi = lax.broadcasted_iota(jnp.int32, (BLOCK, BLOCK), 0)
    coli = lax.broadcasted_iota(jnp.int32, (BLOCK, BLOCK), 1)
    wide = lax.broadcasted_iota(jnp.int32, (BLOCK, size), 1)

    def step(k, carry):
        start = pl.multiple_of(k * BLOCK, BLOCK)
        here = pl.ds(start, BLOCK)
        tiles = [
            work[pl.ds(pl.multiple_of(start + 8 * p, 8), 8), here] for p in range(BLOCK // 8)
        ]
        tiles = pivot_block(tiles)
        own = jnp.where(rowi >= coli, jnp.concatenate(tiles, axis=0), 0.0)
        rows = matmul(own, work[here, :], ((1,), (0,)))
        work[here, :] = rows
        work[here, here] = own
        rows = work[here, :]
        work[:, here] = jnp.where(
            lax.broadcasted_iota(jnp.int32, (size, BLOCK), 0) >= start + BLOCK, 0.0, work[:, here]
        )
        left = jnp.where(wide >= start + BLOCK, rows, 0.0)
        work[...] = work[...] - matmul(left, rows, ((0,), (0,)))
        work[here, :] = jnp.where(wide < start + BLOCK, rows, 0.0)
        return carry

    lax.fori_loop(0, size // BLOCK, step, 0)


def add_ridge(gram, sketch_total):
    size = gram.shape[0]
    rowi = lax.broadcasted_iota(jnp.int32, (size, size), 0)
    coli = lax.broadcasted_iota(jnp.int32, (size, size), 1)
    return gram / sketch_total + jnp.where(rowi == coli, 0.001, 0.0)


def halves(value):
    high = value.astype(jnp.bfloat16)
    return high, (value - high.astype(jnp.float32)).astype(jnp.bfloat16)


def split_matmul(a, b, dims):
    dot = functools.partial(
        lax.dot_general, dimension_numbers=(dims, ((), ())), preferred_element_type=jnp.float32
    )
    return dot(a[0], b[0]) + (dot(a[0], b[1]) + dot(a[1], b[0]))


def finish(work, panel_ref, out_ref):
    rows, columns = panel_ref.shape
    part = columns // 2
    for base in (0, part):
        deep = base + part
        factor = halves(work[base : base + part, 0:deep])
        out_ref[:, base : base + part] = split_matmul(
            halves(panel_ref[:, 0:deep]), factor, ((1,), (1,))
        )


def gram_kernel(sketch_total, sketch_ref, panel_ref, own_ref, out_ref, work):
    own_ref[...] = sketch_ref[0 : own_ref.shape[0], :]
    sketch = halves(sketch_ref[...])
    work[...] = add_ridge(split_matmul(sketch, sketch, ((0,), (0,))), sketch_total)
    inverse_factor(work)
    finish(work, panel_ref, out_ref)


def from_gram_kernel(sketch_total, gram_ref, panel_ref, out_ref, work):
    work[...] = add_ridge(gram_ref[...], sketch_total)
    inverse_factor(work)
    finish(work, panel_ref, out_ref)


def flip(index, mask):
    bit = 1
    while bit <= mask:
        if mask & bit:
            index = index + bit - 2 * bit * lax.rem(lax.div(index, bit), 2)
        bit = 2 * bit
    return index


def parity_sign(value, bits):
    span = 1
    while span < bits:
        span = span * 2
    while span > 1:
        span = span // 2
        value = value ^ (value >> span)
    return (1 - 2 * (value & 1)).astype(jnp.float32)


def sketch_kernel(
    groups, per_owner, scale, panel_ref, signs_ref, group_ref, row_ref, whole_ref,
    lists, values, high, low, choice, acc, from_core, from_first, from_second, from_group, send, recv,
):
    devices = 8
    rows_here, columns = panel_ref.shape
    part = columns // 4
    lefts, rights = (pl.ds(0, part), pl.ds(2 * part, part)), (pl.ds(part, part), pl.ds(3 * part, part))
    both = (pl.ds(0, 2 * part), pl.ds(2 * part, 2 * part))
    band = groups * devices * per_owner
    share = devices * per_owner
    me = lax.axis_index("dev")
    here = lax.axis_index("grp")

    barrier = pltpu.get_barrier_semaphore()
    for mask in range(1, devices):
        pl.semaphore_signal(
            barrier, inc=1, device_id={"dev": flip(me, mask)}, device_id_type=pl.DeviceIdType.MESH
        )
    for mask in range(1, groups):
        pl.semaphore_signal(
            barrier, inc=1, device_id={"grp": flip(here, mask)}, device_id_type=pl.DeviceIdType.MESH
        )
    pl.semaphore_wait(barrier, devices + groups - 2)

    taken = []

    def transfer(source, target, axis, mask):
        place = len(taken)
        taken.append(place)
        peer = flip(me if axis == "dev" else here, mask)
        copy = pltpu.make_async_remote_copy(
            src_ref=source,
            dst_ref=target,
            send_sem=send.at[place],
            recv_sem=recv.at[place],
            device_id={axis: peer},
            device_id_type=pl.DeviceIdType.MESH,
        )
        copy.start()
        return copy

    sends = []
    listed = [transfer(group_ref, lists.at[0, mask], "dev", mask) for mask in range(1, devices)]
    listed += [transfer(row_ref, lists.at[1, mask], "dev", mask) for mask in range(1, devices)]
    top = panel_ref[...].astype(jnp.bfloat16)
    high[...] = top
    low[...] = (panel_ref[...] - top.astype(jnp.float32)).astype(jnp.bfloat16)
    lists[0, 0] = group_ref[...]
    lists[1, 0] = row_ref[...]
    for copy in listed:
        copy.wait_recv()
    sends += listed

    for slot in range(devices):
        values[slot * groups : (slot + 1) * groups, :] = (
            lists[0, slot] * devices + flip(me, slot)
        ) * rows_here + lists[1, slot]
    total = devices * band
    width = devices * per_owner
    place = lax.broadcasted_iota(jnp.int32, (total, width), 0)
    entry = lax.broadcasted_iota(jnp.int32, (total, width), 1)
    wanted = ((place // band) ^ me) * per_owner + place % per_owner
    spread = lax.dot_general(
        (entry == wanted).astype(jnp.float32),
        values[...].astype(jnp.float32),
        (((1,), (1,)), ((), ())),
        precision=lax.Precision.HIGHEST,
        preferred_element_type=jnp.float32,
    )
    place = lax.broadcasted_iota(jnp.int32, (total, devices * groups), 0)
    held = lax.broadcasted_iota(jnp.int32, (total, devices * groups), 1)
    source = (((place // per_owner) % devices) ^ me) * groups + (((place // share) % groups) ^ here)
    choice[...] = jnp.sum(jnp.where(held == source, spread, 0.0), axis=1, keepdims=True).astype(jnp.int32)

    def mixed(chunk):
        pick = jnp.broadcast_to(choice[chunk * band : (chunk + 1) * band, :], (band, 128))
        lane = lax.broadcasted_iota(jnp.int32, (band, 128), 1)
        rank = here * devices + me
        above = parity_sign((pick // rows_here) & rank, (groups * devices).bit_length() - 1)
        table = [parity_sign(pick & lane, 7) * above]
        bit = 7
        while 128 * len(table) < rows_here:
            turn = (1 - 2 * ((pick >> bit) & 1)).astype(jnp.float32)
            table = table + [part * turn for part in table]
            bit = bit + 1
        turns = (1 - 2 * signs_ref[...]).astype(jnp.float32)
        table = [part * turns[i : i + 1, :] for i, part in enumerate(table)]
        table = jnp.concatenate([part.astype(jnp.bfloat16) for part in table], axis=1)
        dims = (((1,), (0,)), ((), ()))
        return lax.dot_general(
            table, high[...], dims, preferred_element_type=jnp.float32
        ) + lax.dot_general(table, low[...], dims, preferred_element_type=jnp.float32)

    core = {}
    for chunk in (7, 3, 5, 1):
        acc[chunk] = mixed(chunk)
        core[chunk - 1] = transfer(acc.at[chunk], from_core.at[chunk // 2], "dev", 1)
    first, second = {}, {}

    def send_first(chunk, turn):
        left, right = lefts[turn], rights[turn]
        if chunk & 2:
            first[turn, "left", chunk - 2] = transfer(
                acc.at[chunk, :, left], from_first.at[chunk // 4, :, left], "dev", 2
            )
        if chunk & 4:
            first[turn, "right", chunk - 4] = transfer(
                acc.at[chunk, :, right], from_first.at[(chunk & 2) // 2, :, right], "dev", 4
            )

    for chunk in (6, 2, 4, 0):
        acc[chunk] = mixed(chunk)
        core[chunk].wait_recv()
        acc[chunk] = acc[chunk] + from_core[chunk // 2]
        send_first(chunk, 0)
        if chunk == 4:
            for late in (6, 2, 4):
                send_first(late, 1)
    for turn in range(2):
        left, right = lefts[turn], rights[turn]
        first[turn, "left", 4].wait_recv()
        acc[4, :, left] = acc[4, :, left] + from_first[1, :, left]
        second[turn, "left"] = transfer(acc.at[4, :, left], from_second.at[:, left], "dev", 4)
        first[turn, "right", 2].wait_recv()
        acc[2, :, right] = acc[2, :, right] + from_first[1, :, right]
        second[turn, "right"] = transfer(acc.at[2, :, right], from_second.at[:, right], "dev", 2)
    summed = []
    for turn in range(2):
        first[turn, "left", 0].wait_recv()
        first[turn, "right", 0].wait_recv()
        second[turn, "left"].wait_recv()
        second[turn, "right"].wait_recv()
        columns_now = both[turn]
        acc[0, :, columns_now] = (
            acc[0, :, columns_now] + from_first[0, :, columns_now] + from_second[:, columns_now]
        )
        summed.append([
            transfer(
                acc.at[0, pl.ds(block * share, share), columns_now],
                from_group.at[block, :, columns_now],
                "grp",
                block,
            )
            for block in range(1, groups)
        ])
    sends += list(core.values()) + list(first.values()) + list(second.values())

    spread_out = []
    for turn in range(2):
        columns_now = both[turn]
        result = acc[0, 0:share, columns_now]
        for block in range(1, groups):
            summed[turn][block - 1].wait_recv()
            result = result + from_group[block, :, columns_now]
        whole_ref[0, 0:share, columns_now] = result * scale
        spread_out.append([
            transfer(
                whole_ref.at[0, pl.ds(0, share), columns_now],
                whole_ref.at[0, pl.ds(block * share, share), columns_now],
                "grp",
                block,
            )
            for block in range(1, groups)
        ])
        sends += summed[turn]
    out, relay, last = [], [], []

    def hand_over(chunk, turn):
        columns_now = both[turn]
        last.append(
            transfer(whole_ref.at[chunk, :, columns_now], whole_ref.at[chunk + 1, :, columns_now], "dev", 1)
        )

    for turn in range(2):
        left, right = lefts[turn], rights[turn]
        for copy in spread_out[turn]:
            copy.wait_recv()
        out.append([
            transfer(whole_ref.at[0, :, left], whole_ref.at[4, :, left], "dev", 4),
            transfer(whole_ref.at[0, :, right], whole_ref.at[2, :, right], "dev", 2),
            transfer(whole_ref.at[0, :, left], whole_ref.at[2, :, left], "dev", 2),
            transfer(whole_ref.at[0, :, right], whole_ref.at[4, :, right], "dev", 4),
        ])
        hand_over(0, turn)
        sends += spread_out[turn] + out[turn]
    for turn in range(2):
        left, right = lefts[turn], rights[turn]
        out[turn][0].wait_recv()
        relay.append(transfer(whole_ref.at[4, :, left], whole_ref.at[6, :, left], "dev", 2))
        out[turn][1].wait_recv()
        relay.append(transfer(whole_ref.at[2, :, right], whole_ref.at[6, :, right], "dev", 4))
        out[turn][2].wait_recv()
        hand_over(2, turn)
        out[turn][3].wait_recv()
        hand_over(4, turn)
    for turn in range(2):
        relay[2 * turn].wait_recv()
        relay[2 * turn + 1].wait_recv()
        hand_over(6, turn)
    for copy in last:
        copy.wait_recv()
    sends += relay + last
    for copy in sends:
        copy.wait_send()


def kernel_sketch(panel, signs, source_group, source_row, groups, devices):
    rows_here, columns = panel.shape
    per_owner = source_row.shape[2] // devices
    band = groups * devices * per_owner
    share = devices * per_owner
    scale = 1.0 / math.sqrt(rows_here * devices * groups)
    vmem = pl.BlockSpec(memory_space=pltpu.VMEM)
    f32 = jnp.float32
    whole = pl.pallas_call(
        functools.partial(sketch_kernel, groups, per_owner, scale),
        out_shape=jax.ShapeDtypeStruct((devices, band, columns), f32),
        in_specs=[vmem] * 4,
        out_specs=vmem,
        scratch_shapes=[
            pltpu.VMEM((2, devices, groups, share), jnp.int32),
            pltpu.VMEM((devices * groups, share), jnp.int32),
            pltpu.VMEM((rows_here, columns), jnp.bfloat16),
            pltpu.VMEM((rows_here, columns), jnp.bfloat16),
            pltpu.VMEM((devices * band, 1), jnp.int32),
            pltpu.VMEM((devices, band, columns), f32),
            pltpu.VMEM((devices // 2, band, columns), f32),
            pltpu.VMEM((2, band, columns), f32),
            pltpu.VMEM((band, columns), f32),
            pltpu.VMEM((groups, share, columns), f32),
            pltpu.SemaphoreType.DMA((72,)),
            pltpu.SemaphoreType.DMA((72,)),
        ],
        compiler_params=pltpu.CompilerParams(collective_id=0, has_side_effects=True),
        name="sketch",
    )(
        panel,
        signs.reshape(rows_here // 128, 128),
        source_group.reshape(groups, share),
        source_row.reshape(groups, share),
    )
    return whole.reshape(devices * band, columns)


def bit_parity(value, bits):
    total = jnp.zeros_like(value)
    for bit_place in range(bits):
        total = total + (value >> bit_place & 1)
    return total & 1


def sylvester(order):
    index = jnp.arange(order, dtype=jnp.int32)
    parity = bit_parity(index[:, None] & index[None, :], order.bit_length())
    return (1 - 2 * parity).astype(jnp.float32)


def general_sketch(panel, signs, source_group, source_row):
    rows_here = panel.shape[0]
    columns = panel.shape[1]
    groups = lax.axis_size("grp")
    devices = lax.axis_size("dev")
    group_here = lax.axis_index("grp")
    highest = lax.Precision.HIGHEST
    flipped = panel * (1 - 2 * signs).astype(jnp.float32)[:, None]
    local = jnp.dot(
        sylvester(rows_here), flipped, precision=highest, preferred_element_type=jnp.float32
    )
    dev_table = sylvester(devices)
    mixed = jnp.einsum(
        "ed,dbc->ebc",
        dev_table,
        lax.all_to_all(
            local.reshape(devices, rows_here // devices, columns),
            "dev",
            split_axis=0,
            concat_axis=0,
            tiled=True,
        ),
        precision=highest,
    )
    inner = mixed
    inner = inner.reshape(rows_here, columns)
    chosen_group = source_group[:, 0, :, 0]
    chosen_row = source_row[:, 0, :]
    width = chosen_group.shape[1]
    per_owner = width // devices
    band_size = rows_here // devices
    dev_here = lax.axis_index("dev")
    stacked = jnp.stack([chosen_group, chosen_row]).reshape(2, groups, devices, per_owner)
    lists = lax.all_to_all(stacked, "dev", split_axis=2, concat_axis=2, tiled=True)
    band_group = lists[0].reshape(-1)
    band_row = lists[1].reshape(-1)
    flat_place = jnp.arange(groups * devices * per_owner, dtype=jnp.int32)
    source_dev = flat_place // per_owner % devices
    flat_index = source_dev * band_size + band_row - dev_here * band_size
    parity = bit_parity(band_group & group_here, groups.bit_length())
    factor = (1 - 2 * parity).astype(jnp.float32)
    gathered = lax.psum_scatter(
        inner[flat_index] * factor[:, None], "grp", scatter_dimension=0, tiled=True
    )
    panel_total = rows_here * devices * groups
    sketch = gathered * (1.0 / math.sqrt(panel_total))
    sketch_total = sketch.shape[0] * devices * groups
    partial_gram = jnp.dot(sketch.T, sketch, precision=highest, preferred_element_type=jnp.float32)
    return sketch, lax.psum(partial_gram, ("grp", "dev"))


def on_device(panel, signs, source_group, source_row):
    rows_here, columns = panel.shape
    groups = lax.axis_size("grp")
    devices = lax.axis_size("dev")
    width = source_row.shape[2]
    sketch_total = groups * devices * width
    fits = groups & (groups - 1) == 0 and groups * width == 128 and columns % 512 == 0 and rows_here % 128 == 0
    if devices == 8 and fits and rows_here & (rows_here - 1) == 0:
        pieces = kernel_sketch(panel, signs, source_group, source_row, groups, devices)
        kernel, shapes = gram_kernel, [(width, columns), (rows_here, columns)]
    else:
        sketch, pieces = general_sketch(panel, signs, source_group, source_row)
        kernel, shapes = from_gram_kernel, [(rows_here, columns)]
    *own, conditioned = pl.pallas_call(
        functools.partial(kernel, sketch_total),
        out_shape=[jax.ShapeDtypeStruct(shape, jnp.float32) for shape in shapes],
        in_specs=[pl.BlockSpec(memory_space=pltpu.VMEM)] * 2,
        out_specs=[pl.BlockSpec(memory_space=pltpu.VMEM)] * len(shapes),
        scratch_shapes=[pltpu.VMEM((columns, columns), jnp.float32)],
        name="factor",
    )(pieces, panel)
    if own:
        sketch = own[0]
    return (sketch, conditioned)


def solution(mesh):
    return jax.shard_map(
        on_device,
        mesh=mesh,
        in_specs=(
            P(("grp", "dev"), None),
            P(("grp", "dev")),
            P(None, "dev", None, None),
            P(None, "dev", None),
        ),
        out_specs=(P(("grp", "dev"), None), P(("grp", "dev"), None)),
        check_vma=False,
    )
```

```python
import functools
import math
import jax
import jax.numpy as jnp
from jax import lax
from jax.experimental import pallas as pl
from jax.experimental.pallas import tpu as pltpu
from jax.sharding import PartitionSpec as P

BLOCK = 128


def pivot_block(tiles):
    count = len(tiles)
    lane = lax.broadcasted_iota(jnp.int32, (8, BLOCK), 1)
    sub = lax.broadcasted_iota(jnp.int32, (8, BLOCK), 0)
    tiles = list(tiles)
    for p in range(count):
        base = 8 * p
        inside = (lane >= base) & (lane < base + 8)
        cols = {
            q: [jnp.broadcast_to(tiles[q][:, base + t : base + t + 1], (8, BLOCK)) for t in range(8)]
            for q in range(p, count)
        }
        tiles[p] = jnp.where(inside, (lane - base == sub).astype(jnp.float32), tiles[p])
        for q in range(p + 1, count):
            tiles[q] = jnp.where(inside, 0.0, tiles[q])
        diag = jnp.ones((8, BLOCK), jnp.float32)
        for t in range(8):
            pivot = jnp.broadcast_to(cols[p][t][t : t + 1, :], (8, BLOCK))
            diag = jnp.where(sub == t, pivot, diag)
            inverse = 1.0 / pivot
            row = jnp.broadcast_to(tiles[p][t : t + 1, :], (8, BLOCK)) * inverse
            heads = [
                jnp.broadcast_to(cols[p][u][t : t + 1, :], (8, BLOCK)) * inverse for u in range(t + 1, 8)
            ]
            for q in range(p, count):
                coef = cols[q][t]
                if q == p:
                    coef = jnp.where(sub > t, coef, 0.0)
                for place, u in enumerate(range(t + 1, 8)):
                    cols[q][u] = cols[q][u] - coef * heads[place]
                tiles[q] = tiles[q] - coef * row
        tiles[p] = tiles[p] * lax.rsqrt(diag)
    return tiles


def inverse_factor(work):
    size = work.shape[0]
    rowi = lax.broadcasted_iota(jnp.int32, (BLOCK, BLOCK), 0)
    coli = lax.broadcasted_iota(jnp.int32, (BLOCK, BLOCK), 1)
    wide = lax.broadcasted_iota(jnp.int32, (BLOCK, size), 1)

    def step(k, carry):
        start = pl.multiple_of(k * BLOCK, BLOCK)
        here = pl.ds(start, BLOCK)
        tiles = [
            work[pl.ds(pl.multiple_of(start + 8 * p, 8), 8), here] for p in range(BLOCK // 8)
        ]
        tiles = pivot_block(tiles)
        own = jnp.where(rowi >= coli, jnp.concatenate(tiles, axis=0), 0.0)
        rows = split_matmul(halves(own), halves(work[here, :]), ((1,), (0,)))
        work[here, :] = rows
        work[here, here] = own
        rows = work[here, :]

        @pl.when(start + BLOCK < size)
        def _():
            work[:, here] = jnp.where(
                lax.broadcasted_iota(jnp.int32, (size, BLOCK), 0) >= start + BLOCK, 0.0, work[:, here]
            )
            left = jnp.where(wide >= start + BLOCK, rows, 0.0)
            work[...] = work[...] - split_matmul(halves(left), halves(rows), ((0,), (0,)))

        work[here, :] = jnp.where(wide < start + BLOCK, rows, 0.0)
        return carry

    lax.fori_loop(0, size // BLOCK, step, 0)


def add_ridge(gram, sketch_total):
    size = gram.shape[0]
    rowi = lax.broadcasted_iota(jnp.int32, (size, size), 0)
    coli = lax.broadcasted_iota(jnp.int32, (size, size), 1)
    return gram / sketch_total + jnp.where(rowi == coli, 0.001, 0.0)


def halves(value):
    high = value.astype(jnp.bfloat16)
    return high, (value - high.astype(jnp.float32)).astype(jnp.bfloat16)


def split_matmul(a, b, dims):
    dot = functools.partial(
        lax.dot_general, dimension_numbers=(dims, ((), ())), preferred_element_type=jnp.float32
    )
    return dot(a[0], b[0]) + (dot(a[0], b[1]) + dot(a[1], b[0]))


def finish(work, panel_ref, out_ref):
    rows, columns = panel_ref.shape
    part = columns // 2
    for base in (0, part):
        deep = base + part
        factor = halves(work[base : base + part, 0:deep])
        out_ref[:, base : base + part] = split_matmul(
            halves(panel_ref[:, 0:deep]), factor, ((1,), (1,))
        )


def gram_kernel(sketch_total, sketch_ref, panel_ref, own_ref, out_ref, work):
    own_ref[...] = sketch_ref[0 : own_ref.shape[0], :]
    sketch = halves(sketch_ref[...])
    work[...] = add_ridge(split_matmul(sketch, sketch, ((0,), (0,))), sketch_total)
    inverse_factor(work)
    finish(work, panel_ref, out_ref)


def from_gram_kernel(sketch_total, gram_ref, panel_ref, out_ref, work):
    work[...] = add_ridge(gram_ref[...], sketch_total)
    inverse_factor(work)
    finish(work, panel_ref, out_ref)


def flip(index, mask):
    bit = 1
    while bit <= mask:
        if mask & bit:
            index = index + bit - 2 * bit * lax.rem(lax.div(index, bit), 2)
        bit = 2 * bit
    return index


def parity_sign(value, bits):
    span = 1
    while span < bits:
        span = span * 2
    while span > 1:
        span = span // 2
        value = value ^ (value >> span)
    return (1 - 2 * (value & 1)).astype(jnp.float32)


def sketch_kernel(
    groups, per_owner, scale, panel_ref, signs_ref, group_ref, row_ref, whole_ref,
    lists, values, high, low, choice, acc, from_core, from_first, from_second, from_group, send, recv,
):
    devices = 8
    rows_here, columns = panel_ref.shape
    part = columns // 4
    lefts, rights = (pl.ds(0, part), pl.ds(2 * part, part)), (pl.ds(part, part), pl.ds(3 * part, part))
    both = (pl.ds(0, 2 * part), pl.ds(2 * part, 2 * part))
    band = groups * devices * per_owner
    share = devices * per_owner
    me = lax.axis_index("dev")
    here = lax.axis_index("grp")

    barrier = pltpu.get_barrier_semaphore()
    for mask in range(1, devices):
        pl.semaphore_signal(
            barrier, inc=1, device_id={"dev": flip(me, mask)}, device_id_type=pl.DeviceIdType.MESH
        )
    for mask in range(1, groups):
        pl.semaphore_signal(
            barrier, inc=1, device_id={"grp": flip(here, mask)}, device_id_type=pl.DeviceIdType.MESH
        )
    pl.semaphore_wait(barrier, devices + groups - 2)

    taken = []

    def transfer(source, target, axis, mask):
        place = len(taken)
        taken.append(place)
        peer = flip(me if axis == "dev" else here, mask)
        copy = pltpu.make_async_remote_copy(
            src_ref=source,
            dst_ref=target,
            send_sem=send.at[place],
            recv_sem=recv.at[place],
            device_id={axis: peer},
            device_id_type=pl.DeviceIdType.MESH,
        )
        copy.start()
        return copy

    sends = []
    listed = [transfer(group_ref, lists.at[0, mask], "dev", mask) for mask in range(1, devices)]
    listed += [transfer(row_ref, lists.at[1, mask], "dev", mask) for mask in range(1, devices)]
    top = panel_ref[...].astype(jnp.bfloat16)
    high[...] = top
    low[...] = (panel_ref[...] - top.astype(jnp.float32)).astype(jnp.bfloat16)
    lists[0, 0] = group_ref[...]
    lists[1, 0] = row_ref[...]
    for copy in listed:
        copy.wait_recv()
    sends += listed

    for slot in range(devices):
        values[slot * groups : (slot + 1) * groups, :] = (
            lists[0, slot] * devices + flip(me, slot)
        ) * rows_here + lists[1, slot]
    total = devices * band
    width = devices * per_owner
    place = lax.broadcasted_iota(jnp.int32, (total, width), 0)
    entry = lax.broadcasted_iota(jnp.int32, (total, width), 1)
    wanted = ((place // band) ^ me) * per_owner + place % per_owner
    spread = lax.dot_general(
        (entry == wanted).astype(jnp.float32),
        values[...].astype(jnp.float32),
        (((1,), (1,)), ((), ())),
        precision=lax.Precision.HIGHEST,
        preferred_element_type=jnp.float32,
    )
    place = lax.broadcasted_iota(jnp.int32, (total, devices * groups), 0)
    held = lax.broadcasted_iota(jnp.int32, (total, devices * groups), 1)
    source = (((place // per_owner) % devices) ^ me) * groups + (((place // share) % groups) ^ here)
    choice[...] = jnp.sum(jnp.where(held == source, spread, 0.0), axis=1, keepdims=True).astype(jnp.int32)

    def mixed(chunk):
        pick = jnp.broadcast_to(choice[chunk * band : (chunk + 1) * band, :], (band, 128))
        lane = lax.broadcasted_iota(jnp.int32, (band, 128), 1)
        rank = here * devices + me
        above = parity_sign((pick // rows_here) & rank, (groups * devices).bit_length() - 1)
        table = [parity_sign(pick & lane, 7) * above]
        bit = 7
        while 128 * len(table) < rows_here:
            turn = (1 - 2 * ((pick >> bit) & 1)).astype(jnp.float32)
            table = table + [part * turn for part in table]
            bit = bit + 1
        turns = (1 - 2 * signs_ref[...]).astype(jnp.float32)
        table = [part * turns[i : i + 1, :] for i, part in enumerate(table)]
        table = jnp.concatenate([part.astype(jnp.bfloat16) for part in table], axis=1)
        dims = (((1,), (0,)), ((), ()))
        return lax.dot_general(
            table, high[...], dims, preferred_element_type=jnp.float32
        ) + lax.dot_general(table, low[...], dims, preferred_element_type=jnp.float32)

    core = {}
    for chunk in (7, 3, 5, 1):
        acc[chunk] = mixed(chunk)
        core[chunk - 1] = transfer(acc.at[chunk], from_core.at[chunk // 2], "dev", 1)
    first, second = {}, {}

    def send_first(chunk, turn):
        left, right = lefts[turn], rights[turn]
        if chunk & 2:
            first[turn, "left", chunk - 2] = transfer(
                acc.at[chunk, :, left], from_first.at[chunk // 4, :, left], "dev", 2
            )
        if chunk & 4:
            first[turn, "right", chunk - 4] = transfer(
                acc.at[chunk, :, right], from_first.at[(chunk & 2) // 2, :, right], "dev", 4
            )

    for chunk in (6, 2, 4, 0):
        acc[chunk] = mixed(chunk)
        core[chunk].wait_recv()
        acc[chunk] = acc[chunk] + from_core[chunk // 2]
        send_first(chunk, 0)
        if chunk == 4:
            for late in (6, 2, 4):
                send_first(late, 1)
    for turn in range(2):
        left, right = lefts[turn], rights[turn]
        first[turn, "left", 4].wait_recv()
        acc[4, :, left] = acc[4, :, left] + from_first[1, :, left]
        second[turn, "left"] = transfer(acc.at[4, :, left], from_second.at[:, left], "dev", 4)
        first[turn, "right", 2].wait_recv()
        acc[2, :, right] = acc[2, :, right] + from_first[1, :, right]
        second[turn, "right"] = transfer(acc.at[2, :, right], from_second.at[:, right], "dev", 2)
    summed = []
    for turn in range(2):
        first[turn, "left", 0].wait_recv()
        first[turn, "right", 0].wait_recv()
        second[turn, "left"].wait_recv()
        second[turn, "right"].wait_recv()
        columns_now = both[turn]
        acc[0, :, columns_now] = (
            acc[0, :, columns_now] + from_first[0, :, columns_now] + from_second[:, columns_now]
        )
        summed.append([
            transfer(
                acc.at[0, pl.ds(block * share, share), columns_now],
                from_group.at[block, :, columns_now],
                "grp",
                block,
            )
            for block in range(1, groups)
        ])
    sends += list(core.values()) + list(first.values()) + list(second.values())

    spread_out = []
    for turn in range(2):
        columns_now = both[turn]
        result = acc[0, 0:share, columns_now]
        for block in range(1, groups):
            summed[turn][block - 1].wait_recv()
            result = result + from_group[block, :, columns_now]
        whole_ref[0, 0:share, columns_now] = result * scale
        spread_out.append([
            transfer(
                whole_ref.at[0, pl.ds(0, share), columns_now],
                whole_ref.at[0, pl.ds(block * share, share), columns_now],
                "grp",
                block,
            )
            for block in range(1, groups)
        ])
        sends += summed[turn]
    out, relay, last = [], [], []

    def hand_over(chunk, turn):
        columns_now = both[turn]
        last.append(
            transfer(whole_ref.at[chunk, :, columns_now], whole_ref.at[chunk + 1, :, columns_now], "dev", 1)
        )

    for turn in range(2):
        left, right = lefts[turn], rights[turn]
        for copy in spread_out[turn]:
            copy.wait_recv()
        out.append([
            transfer(whole_ref.at[0, :, left], whole_ref.at[4, :, left], "dev", 4),
            transfer(whole_ref.at[0, :, right], whole_ref.at[2, :, right], "dev", 2),
            transfer(whole_ref.at[0, :, left], whole_ref.at[2, :, left], "dev", 2),
            transfer(whole_ref.at[0, :, right], whole_ref.at[4, :, right], "dev", 4),
        ])
        hand_over(0, turn)
        sends += spread_out[turn] + out[turn]
    for turn in range(2):
        left, right = lefts[turn], rights[turn]
        out[turn][0].wait_recv()
        relay.append(transfer(whole_ref.at[4, :, left], whole_ref.at[6, :, left], "dev", 2))
        out[turn][1].wait_recv()
        relay.append(transfer(whole_ref.at[2, :, right], whole_ref.at[6, :, right], "dev", 4))
        out[turn][2].wait_recv()
        hand_over(2, turn)
        out[turn][3].wait_recv()
        hand_over(4, turn)
    for turn in range(2):
        relay[2 * turn].wait_recv()
        relay[2 * turn + 1].wait_recv()
        hand_over(6, turn)
    for copy in last:
        copy.wait_recv()
    sends += relay + last
    for copy in sends:
        copy.wait_send()


def kernel_sketch(panel, signs, source_group, source_row, groups, devices):
    rows_here, columns = panel.shape
    per_owner = source_row.shape[2] // devices
    band = groups * devices * per_owner
    share = devices * per_owner
    scale = 1.0 / math.sqrt(rows_here * devices * groups)
    vmem = pl.BlockSpec(memory_space=pltpu.VMEM)
    f32 = jnp.float32
    whole = pl.pallas_call(
        functools.partial(sketch_kernel, groups, per_owner, scale),
        out_shape=jax.ShapeDtypeStruct((devices, band, columns), f32),
        in_specs=[vmem] * 4,
        out_specs=vmem,
        scratch_shapes=[
            pltpu.VMEM((2, devices, groups, share), jnp.int32),
            pltpu.VMEM((devices * groups, share), jnp.int32),
            pltpu.VMEM((rows_here, columns), jnp.bfloat16),
            pltpu.VMEM((rows_here, columns), jnp.bfloat16),
            pltpu.VMEM((devices * band, 1), jnp.int32),
            pltpu.VMEM((devices, band, columns), f32),
            pltpu.VMEM((devices // 2, band, columns), f32),
            pltpu.VMEM((2, band, columns), f32),
            pltpu.VMEM((band, columns), f32),
            pltpu.VMEM((groups, share, columns), f32),
            pltpu.SemaphoreType.DMA((72,)),
            pltpu.SemaphoreType.DMA((72,)),
        ],
        compiler_params=pltpu.CompilerParams(collective_id=0, has_side_effects=True),
        name="sketch",
    )(
        panel,
        signs.reshape(rows_here // 128, 128),
        source_group.reshape(groups, share),
        source_row.reshape(groups, share),
    )
    return whole.reshape(devices * band, columns)


def bit_parity(value, bits):
    total = jnp.zeros_like(value)
    for bit_place in range(bits):
        total = total + (value >> bit_place & 1)
    return total & 1


def sylvester(order):
    index = jnp.arange(order, dtype=jnp.int32)
    parity = bit_parity(index[:, None] & index[None, :], order.bit_length())
    return (1 - 2 * parity).astype(jnp.float32)


def general_sketch(panel, signs, source_group, source_row):
    rows_here = panel.shape[0]
    columns = panel.shape[1]
    groups = lax.axis_size("grp")
    devices = lax.axis_size("dev")
    group_here = lax.axis_index("grp")
    highest = lax.Precision.HIGHEST
    flipped = panel * (1 - 2 * signs).astype(jnp.float32)[:, None]
    local = jnp.dot(
        sylvester(rows_here), flipped, precision=highest, preferred_element_type=jnp.float32
    )
    dev_table = sylvester(devices)
    mixed = jnp.einsum(
        "ed,dbc->ebc",
        dev_table,
        lax.all_to_all(
            local.reshape(devices, rows_here // devices, columns),
            "dev",
            split_axis=0,
            concat_axis=0,
            tiled=True,
        ),
        precision=highest,
    )
    inner = mixed
    inner = inner.reshape(rows_here, columns)
    chosen_group = source_group[:, 0, :, 0]
    chosen_row = source_row[:, 0, :]
    width = chosen_group.shape[1]
    per_owner = width // devices
    band_size = rows_here // devices
    dev_here = lax.axis_index("dev")
    stacked = jnp.stack([chosen_group, chosen_row]).reshape(2, groups, devices, per_owner)
    lists = lax.all_to_all(stacked, "dev", split_axis=2, concat_axis=2, tiled=True)
    band_group = lists[0].reshape(-1)
    band_row = lists[1].reshape(-1)
    flat_place = jnp.arange(groups * devices * per_owner, dtype=jnp.int32)
    source_dev = flat_place // per_owner % devices
    flat_index = source_dev * band_size + band_row - dev_here * band_size
    parity = bit_parity(band_group & group_here, groups.bit_length())
    factor = (1 - 2 * parity).astype(jnp.float32)
    gathered = lax.psum_scatter(
        inner[flat_index] * factor[:, None], "grp", scatter_dimension=0, tiled=True
    )
    panel_total = rows_here * devices * groups
    sketch = gathered * (1.0 / math.sqrt(panel_total))
    sketch_total = sketch.shape[0] * devices * groups
    partial_gram = jnp.dot(sketch.T, sketch, precision=highest, preferred_element_type=jnp.float32)
    return sketch, lax.psum(partial_gram, ("grp", "dev"))


def on_device(panel, signs, source_group, source_row):
    rows_here, columns = panel.shape
    groups = lax.axis_size("grp")
    devices = lax.axis_size("dev")
    width = source_row.shape[2]
    sketch_total = groups * devices * width
    fits = groups & (groups - 1) == 0 and groups * width == 128 and columns % 512 == 0 and rows_here % 128 == 0
    if devices == 8 and fits and rows_here & (rows_here - 1) == 0:
        pieces = kernel_sketch(panel, signs, source_group, source_row, groups, devices)
        kernel, shapes = gram_kernel, [(width, columns), (rows_here, columns)]
    else:
        sketch, pieces = general_sketch(panel, signs, source_group, source_row)
        kernel, shapes = from_gram_kernel, [(rows_here, columns)]
    *own, conditioned = pl.pallas_call(
        functools.partial(kernel, sketch_total),
        out_shape=[jax.ShapeDtypeStruct(shape, jnp.float32) for shape in shapes],
        in_specs=[pl.BlockSpec(memory_space=pltpu.VMEM)] * 2,
        out_specs=[pl.BlockSpec(memory_space=pltpu.VMEM)] * len(shapes),
        scratch_shapes=[pltpu.VMEM((columns, columns), jnp.float32)],
        name="factor",
    )(pieces, panel)
    if own:
        sketch = own[0]
    return (sketch, conditioned)


def solution(mesh):
    return jax.shard_map(
        on_device,
        mesh=mesh,
        in_specs=(
            P(("grp", "dev"), None),
            P(("grp", "dev")),
            P(None, "dev", None, None),
            P(None, "dev", None),
        ),
        out_specs=(P(("grp", "dev"), None), P(("grp", "dev"), None)),
        check_vma=False,
    )
```
